32 devices in a mesh: dp: 8 (over y, x, core), mp: 4 (over z).
Axes of the slice: x: 2, y: 2, z: 4, core: 2. Of those that a mesh axis runs over, the one named last changes fastest.
Arguments:
- patches: bfloat16 [1024, 588], P('dp'), may hold values from -6 to 6
- embed_weight: bfloat16 [6144, 588], P(('mp', 'dp')), may hold values from -0.25 to 0.25
- project_weight: bfloat16 [6144, 3, 3072], P('dp', None, 'mp'), may hold values from -0.078125 to 0.078125
- patch_counts: int32 [64], P('dp'), may hold values from 0 to 64, as said below
- segment_ids: int32 [1024], P('dp'), may hold values from -1 to 63, as said below
- targets: bfloat16 [1024, 3072], P('dp', 'mp'), may hold values from -4 to 4
Outputs:
- project_grad: float32 [6144, 3, 3072], P('dp', None, 'mp')
- loss_value: float32 [], replicated
The draws below stay inside these ranges and needn't reach their ends.
Inputs may be any that keep to these rules, and one draw needn't show every extreme that they name: `patch_counts`: entry 8 * i + j is the number of patches of image slot j of device i along dp, a multiple of 16, 0 for an empty slot; the counts of one device add up to at most 128, and some device reaches it. `segment_ids`: the rows of device i along dp hold its images whole, slot after slot, each row carrying the id 8 * i + slot of its image, then -1 on the rows left. A device in the upper half of dp holds more rows than the device half the axis away. On each device the images that end after its row 96 cover at most 64 rows. Those rows plus all the rows of the device half the axis away come to at most 96. Both bounds are reached.
All inputs are finite; a program needn't handle non-finite values.
Results may differ from the reference program's by a relative error of at most 0.012.
The reference program's roundings to bfloat16 on the way (of `embedded`, `normed`, `weights`, `out_grad`, `value_grad` and `score_grad`) count: a program that leaves them out, or rounds other values in their place, can miss the bound.
Values may be sent and summed in bfloat16 or wider, within the bound.
A program may use at most 128 MiB of HBM per device.

```python
import math
import jax
import jax.numpy as jnp
from jax import lax

D = 6144
HEADS = 24
HD = 128
P_SIZE = 588
UNIT = 16
IMGS = 8
CAP = 128
ROWS = 1024
N_DP = 8


def split_units(totals, upper_draws):
    remain = totals
    portions = []
    for column in range(3):
        portion = jnp.minimum(remain, upper_draws[:, column])
        portions.append(portion)
        remain = remain - portion
    portions.append(remain)
    return jnp.stack(portions, axis=1)


def image_layout(key):
    pair_count = N_DP // 2
    base_key = jax.random.fold_in(key, 4242)
    tail_key, head_key, light_key, head_split, tail_split, light_split = jax.random.split(base_key, 6)
    tail_units = jax.random.randint(tail_key, (pair_count,), 2, 5)
    head_units = jnp.minimum(jax.random.randint(head_key, (pair_count,), 4, 6), 8 - tail_units)
    light_units = jax.random.randint(light_key, (pair_count,), 0, 7 - tail_units)
    head_units = head_units.at[0].set(5).at[1].set(4)
    tail_units = tail_units.at[0].set(3).at[1].set(4)
    light_units = light_units.at[0].set(3).at[1].set(2)
    head_parts = split_units(head_units, jax.random.randint(head_split, (pair_count, 4), 1, 5))
    tail_draws = jax.random.randint(tail_split, (pair_count, 4), 1, 5).at[1, 0].set(4)
    tail_parts = split_units(tail_units, tail_draws)
    light_parts = split_units(light_units, jax.random.randint(light_split, (pair_count, 4), 1, 5))
    heavy_side = jnp.concatenate([head_parts, tail_parts], axis=1)
    lighter = jnp.concatenate([light_parts, jnp.zeros_like(light_parts)], axis=1)
    unit_table = jnp.concatenate([lighter, heavy_side], axis=0)
    counts = (unit_table * UNIT).astype(jnp.int32)
    cumulative = jnp.cumsum(counts, axis=1)
    row_load = cumulative[:, -1]
    row_index = jnp.arange(CAP, dtype=jnp.int32)
    slot_index = jnp.sum((cumulative[:, None, :] <= row_index[None, :, None]).astype(jnp.int32), axis=-1)
    device = jnp.arange(N_DP, dtype=jnp.int32)[:, None]
    segment = jnp.where(row_index[None, :] < row_load[:, None], device * IMGS + slot_index, -1)
    return (counts.reshape(-1), segment.reshape(-1).astype(jnp.int32))


def draw_patch_counts(key, part):
    return image_layout(key)[0]


def draw_segment_ids(key, part):
    return image_layout(key)[1]


def level_of(stream_key, shape, pieces, smallest, high):
    level = 1.0
    for dim, shards_of in pieces:
        steps = jax.random.uniform(jax.random.fold_in(jax.random.fold_in(stream_key, 6), dim), (shards_of,), jnp.float32, smallest / len(pieces), high / len(pieces))
        level = level * jnp.repeat(jnp.exp(steps), shape[dim] // shards_of).reshape((-1,) + (1,) * (len(shape) - 1 - dim))
    return level


def normal_values(rng, extent, scale, limit, pieces=(), kind=jnp.bfloat16):
    loudness = level_of(rng, extent, pieces, -0.22, 0.18) if pieces else 1.0
    array = jax.random.normal(rng, extent, jnp.float32) * scale * loudness
    return jnp.minimum(jnp.maximum(array, -limit), limit).astype(kind)


def setup_inputs(seed: int = 0) -> dict:
    key_of = jax.random.split(jax.random.key(seed), 7)
    patches = normal_values(key_of[0], (ROWS, P_SIZE), 1.0, 6.0, ((0, 8),))
    embed_weight = normal_values(key_of[1], (D, P_SIZE), P_SIZE ** -0.5, 0.25, ((0, 32),))
    project_weight = normal_values(key_of[2], (D, 3, HEADS * HD), D ** -0.5, 0.078125, ((0, 8), (2, 4)))
    patch_counts = draw_patch_counts(jax.random.fold_in(key_of[6], 71), 0)
    segment_ids = draw_segment_ids(jax.random.fold_in(key_of[6], 71), 0)
    targets = normal_values(key_of[5], (ROWS, HEADS * HD), 0.5, 4.0, ((0, 8), (1, 4)))
    return dict(patches=patches, embed_weight=embed_weight, project_weight=project_weight, patch_counts=patch_counts, segment_ids=segment_ids, targets=targets)


def layer_norm(values):
    center = values - lax.optimization_barrier(jnp.mean(values, axis=-1, keepdims=True))
    spread = lax.optimization_barrier(jnp.mean(center * center, axis=-1, keepdims=True))
    return center * lax.rsqrt(spread + 1e-06)

def norm_grad(values, cotangent):
    return jax.vjp(layer_norm, values)[1](cotangent)[0]

def attend_block(query_raw, key_raw, value_rows, segment, target):
    inverse_root = 1.0 / math.sqrt(HD)
    query_normed = layer_norm(query_raw).astype(jnp.bfloat16)
    key_normed = layer_norm(key_raw).astype(jnp.bfloat16)
    scores = jnp.einsum('qhd,khd->hqk', query_normed.astype(jnp.float32), key_normed.astype(jnp.float32)) * inverse_root
    valid = segment >= 0
    allowed = (segment[:, None] == segment[None, :]) & valid[:, None]
    exponent = jnp.where(allowed[None], jnp.exp(scores), 0.0)
    denominator = lax.optimization_barrier(jnp.sum(exponent, axis=-1, keepdims=True))
    denominator = jnp.where(valid[None, :, None], denominator, 1.0)
    weights = (exponent / denominator).astype(jnp.bfloat16)
    attended = jnp.einsum('hqk,khd->qhd', weights.astype(jnp.float32), value_rows.astype(jnp.float32))
    feature_count = attended.shape[1] * attended.shape[2]
    error_rows = jnp.where(valid[:, None], attended.reshape(-1, feature_count) - target.astype(jnp.float32), 0.0)
    squared_sum = jnp.sum(error_rows * error_rows)
    return (query_normed, key_normed, weights, error_rows, squared_sum)

def attend_back(query_raw, key_raw, query_normed, key_normed, value_rows, weights, error_rows, patch_total):
    inverse_root = 1.0 / math.sqrt(HD)
    out_grad = (error_rows / patch_total).astype(jnp.bfloat16).reshape(query_normed.shape)
    prob_grad = jnp.einsum('qhd,khd->hqk', out_grad.astype(jnp.float32), value_rows.astype(jnp.float32))
    value_grad = jnp.einsum('hqk,qhd->khd', weights.astype(jnp.float32), out_grad.astype(jnp.float32)).astype(jnp.bfloat16)
    weight_float = weights.astype(jnp.float32)
    score_grad = (weight_float * (prob_grad - lax.optimization_barrier(jnp.sum(prob_grad * weight_float, axis=-1, keepdims=True))) * inverse_root).astype(jnp.bfloat16)
    normed_grad_q = jnp.einsum('hqk,khd->qhd', score_grad.astype(jnp.float32), key_normed.astype(jnp.float32))
    normed_grad_k = jnp.einsum('hqk,qhd->khd', score_grad.astype(jnp.float32), query_normed.astype(jnp.float32))
    query_grad = norm_grad(query_raw, normed_grad_q).astype(jnp.bfloat16)
    key_grad = norm_grad(key_raw, normed_grad_k).astype(jnp.bfloat16)
    return jnp.stack([query_grad, key_grad, value_grad], axis=1)

def reference(patches, embed_weight, project_weight, patch_counts, segment_ids, targets):
    embedded = jnp.dot(patches, embed_weight.T, preferred_element_type=jnp.float32).astype(jnp.bfloat16)
    normed = layer_norm(embedded.astype(jnp.float32)).astype(jnp.bfloat16)
    flat_weight = project_weight.reshape(D, 3 * HEADS * HD)
    projected = jnp.dot(normed, flat_weight, preferred_element_type=jnp.float32).reshape(N_DP, CAP, 3, HEADS, HD)
    patch_total = jnp.sum(patch_counts).astype(jnp.float32)
    segments = segment_ids.reshape(N_DP, CAP)
    target_blocks = targets.reshape(N_DP, CAP, HEADS * HD)

    def per_device(block_item):
        block_data, segment, target = block_item
        query_raw = block_data[:, 0]
        key_raw = block_data[:, 1]
        value_rows = block_data[:, 2].astype(jnp.bfloat16)
        query_normed, key_normed, weights, error_rows, squared_sum = attend_block(query_raw, key_raw, value_rows, segment, target)
        row_grads = attend_back(query_raw, key_raw, query_normed, key_normed, value_rows, weights, error_rows, patch_total)
        return (row_grads, squared_sum)
    row_grads, squared_sums = lax.map(per_device, (projected, segments, target_blocks))
    loss_value = jnp.sum(squared_sums) / (2.0 * patch_total)
    grad_rows = row_grads.reshape(N_DP * CAP, 3 * HEADS * HD)
    project_grad = jnp.dot(normed.T, grad_rows, preferred_element_type=jnp.float32).reshape(D, 3, HEADS * HD)
    return (project_grad, loss_value)
```

```python
import functools
import math

import jax
import jax.numpy as jnp
from jax import lax
from jax.experimental import pallas as pl
from jax.experimental.pallas import tpu as pltpu
from jax.sharding import PartitionSpec as P

HD = 128
MESH = pl.DeviceIdType.MESH
VMEM_BYTES = 62 * 1024 * 1024


def remote(src, dst, send_sem, recv_sem, device_id):
    return pltpu.make_async_remote_copy(
        src_ref=src, dst_ref=dst, send_sem=send_sem, recv_sem=recv_sem,
        device_id=device_id, device_id_type=MESH,
    )


def greet(n, n_mp, d, m):
    barrier = pltpu.get_barrier_semaphore()
    for i in range(1, n):
        pl.semaphore_signal(barrier, inc=1, device_id={"dp": lax.rem(d + i, n)}, device_id_type=MESH)
    for i in range(1, n_mp):
        pl.semaphore_signal(barrier, inc=1, device_id={"mp": lax.rem(m + i, n_mp)}, device_id_type=MESH)
    pl.semaphore_wait(barrier, n - 1 + n_mp - 1)


def project_kernel(
    n, n_mp,
    patches, embed, weight_hbm, counts,
    normed, raw, total,
    pall, zbuf, eblk, wbuf, stats, cbuf, pbuf, pin, sbuf, rbuf,
    w_sem, cs, cr, ps, pr, fs, fr, zs, zr, es, er, ss, sr, bs, br, qs, qr, loc_sem,
):
    d, m = lax.axis_index("dp"), lax.axis_index("mp")
    core, chip = lax.rem(d, 2), d // 2
    partner = d + 1 - 2 * core
    nc, per = n // 2, n // n_mp
    rows = patches.shape[0]
    tile = weight_hbm.shape[2]

    load = pltpu.make_async_copy(weight_hbm, wbuf, w_sem)
    load.start()
    greet(n, n_mp, d, m)

    def peer(i):
        return 2 * lax.rem(chip + i, nc) + core

    def source(i):
        return 2 * lax.rem(chip + nc - i, nc) + core

    def far(i):
        return lax.rem(d + i, n)

    def z_copy(i):
        return remote(embed, zbuf.at[i], zs.at[i], zr.at[i], {"mp": lax.rem(m + i, n_mp)})

    for i in range(1, n_mp):
        z_copy(i).start()

    def c_copy(i):
        return remote(counts, cbuf.at[i], cs.at[i], cr.at[i], {"dp": far(i)})

    def p_copy(i):
        return remote(patches, pall.at[d], ps.at[i], pr.at[i], {"dp": peer(i)})

    def p_own():
        return remote(patches, pall.at[d], ps.at[0], pr.at[0], {"dp": partner})

    def f_copy(i):
        return remote(pall.at[source(i)], pall.at[source(i)], fs.at[i], fr.at[i], {"dp": partner})

    def e_target(i):
        return lax.rem(m + n_mp - i, n_mp) * per + d // n_mp

    def e_copy(i, src):
        return remote(src, eblk.at[lax.rem(d, n_mp)], es.at[i], er.at[lax.rem(d, n_mp)], {"dp": e_target(i)})

    def e_local(i, src):
        return pltpu.make_async_copy(src, eblk.at[lax.rem(d, n_mp)], loc_sem)

    def e_start(i, src):
        @pl.when(e_target(i) != d)
        def _():
            e_copy(i, src).start()

        @pl.when(e_target(i) == d)
        def _():
            e_local(i, src).start()
            e_local(i, src).wait()

    p_own().start()
    for i in range(1, nc):
        p_copy(i).start()
    for i in range(1, n):
        c_copy(i).start()
    e_start(0, embed)
    pall[d] = patches[...]
    for i in range(1, nc):
        p_copy(i).wait_recv()
        f_copy(i).start()
    for i in range(1, n_mp):
        z_copy(i).wait_recv()
        e_start(i, zbuf.at[i])
    sum_counts = counts[...]
    for i in range(1, n):
        c_copy(i).wait_recv()
        sum_counts = sum_counts + cbuf[i]
    total[...] = sum_counts
    p_own().wait_recv()
    for i in range(1, nc):
        f_copy(i).wait_recv()
    for q in range(n_mp):
        origin = lax.rem(d, per) * n_mp + q

        @pl.when(origin != d)
        def _():
            remote(eblk.at[q], eblk.at[q], es.at[q], er.at[q], {"dp": partner}).wait_recv()

    width = eblk.shape[0] * eblk.shape[1]
    feature_total = width * n
    lane = lax.broadcasted_iota(jnp.int32, (rows, 128), 1)

    def embed_block(b, carry):
        block = pall[b]
        parts = jnp.concatenate(
            [eblk[q] for q in range(n_mp)], axis=0
        )
        value = lax.dot_general(
            block, parts, (((1,), (1,)), ((), ())), preferred_element_type=jnp.float32
        ).astype(jnp.bfloat16)
        normed[b] = value
        value = value.astype(jnp.float32)
        mean = jnp.sum(value, axis=-1, keepdims=True) * (1.0 / width)
        center = value - mean
        square = jnp.sum(center * center, axis=-1, keepdims=True)
        both = jnp.where(lane == 0, mean, jnp.where(lane == 1, square, 0.0))
        stats[0, b] = both.T[:8]
        return carry

    lax.fori_loop(0, n, embed_block, 0)

    def s_copy(i):
        return remote(stats.at[0], stats.at[i], ss.at[i], sr.at[i], {"dp": far(i)})

    for i in range(1, n):
        s_copy(i).start()
    for i in range(1, n):
        s_copy(i).wait_recv()

    load.wait()

    def norm_block(b, carry):
        mean = stats[0, b, 0:1, :]
        for i in range(1, n):
            mean = mean + stats[i, b, 0:1, :]
        mean = mean * (1.0 / n)
        square = jnp.zeros_like(mean)
        for i in range(n):
            gap = stats[i, b, 0:1, :] - mean
            square = square + stats[i, b, 1:2, :] + width * (gap * gap)
        scale = lax.rsqrt(square * (1.0 / feature_total) + 1e-06)
        row = lax.broadcasted_iota(jnp.int32, (128, rows), 0)
        both = jnp.where(row == 0, mean, jnp.where(row == 1, scale, 0.0)).T
        value = normed[b].astype(jnp.float32)
        normed[b] = ((value - both[:, 0:1]) * both[:, 1:2]).astype(jnp.bfloat16)
        return carry

    lax.fori_loop(0, n, norm_block, 0)

    def b_copy(i):
        return remote(pbuf.at[i], pin.at[i], bs.at[i], br.at[i], {"dp": partner})

    def q_copy(i):
        return remote(sbuf.at[i], rbuf.at[i], qs.at[i], qr.at[i], {"dp": peer(i)})

    def other_part(k, carry):
        i = lax.rem(k + 1, nc)
        block = normed[2 * lax.rem(chip + i, nc) + 1 - core]
        for s in range(3):
            pbuf[i, :, s * tile:(s + 1) * tile] = jnp.dot(
                block, wbuf[s], preferred_element_type=jnp.float32
            ).astype(jnp.bfloat16)
        b_copy(i).start()
        return carry

    lax.fori_loop(0, nc, other_part, 0)

    def own_part(i, carry):
        block = normed[peer(i)]
        b_copy(i).wait_recv()
        for s in range(3):
            cols = slice(s * tile, (s + 1) * tile)
            sbuf[i, :, cols] = (
                jnp.dot(block, wbuf[s], preferred_element_type=jnp.float32)
                + pin[i, :, cols].astype(jnp.float32)
            ).astype(jnp.bfloat16)
        q_copy(i).start()
        return carry

    lax.fori_loop(1, nc, own_part, 0)
    block = normed[d]
    b_copy(0).wait_recv()
    for s in range(3):
        cols = slice(s * tile, (s + 1) * tile)
        raw[:, cols] = jnp.dot(block, wbuf[s], preferred_element_type=jnp.float32) + pin[
            0, :, cols
        ].astype(jnp.float32)

    def take(i, carry):
        q_copy(i).wait_recv()
        raw[...] += rbuf[i].astype(jnp.float32)
        return carry

    lax.fori_loop(1, nc, take, 0)

    p_own().wait_send()
    for i in range(1, n_mp):
        z_copy(i).wait_send()
    for i in range(n_mp):
        @pl.when(e_target(i) != d)
        def _():
            e_copy(i, embed).wait_send()
    for i in range(1, nc):
        p_copy(i).wait_send()
        f_copy(i).wait_send()
        q_copy(i).wait_send()
    for i in range(nc):
        b_copy(i).wait_send()
    for i in range(1, n):
        c_copy(i).wait_send()
        s_copy(i).wait_send()


def project(patches, embed, weight, counts, n, n_mp):
    rows, width = patches.shape
    pieces = embed.shape[0]
    features, columns = weight.shape[1], 3 * weight.shape[2]
    nc = n // 2
    dma = lambda k: pltpu.SemaphoreType.DMA((k,))
    vmem = pl.BlockSpec(memory_space=pltpu.VMEM)
    bf16, f32 = jnp.bfloat16, jnp.float32
    return pl.pallas_call(
        functools.partial(project_kernel, n, n_mp),
        out_shape=(
            jax.ShapeDtypeStruct((n, rows, features), bf16),
            jax.ShapeDtypeStruct((rows, columns), f32),
            jax.ShapeDtypeStruct((8, 128), f32),
        ),
        in_specs=[vmem, vmem, pl.BlockSpec(memory_space=pl.ANY), vmem],
        out_specs=(vmem, vmem, vmem),
        scratch_shapes=[
            pltpu.VMEM((n, rows, width), bf16),
            pltpu.VMEM((n_mp, pieces, width), bf16),
            pltpu.VMEM((n_mp, pieces, width), bf16),
            pltpu.VMEM(weight.shape, bf16),
            pltpu.VMEM((n, n, 8, rows), f32),
            pltpu.VMEM((n, 8, 128), f32),
            pltpu.VMEM((nc, rows, columns), bf16),
            pltpu.VMEM((nc, rows, columns), bf16),
            pltpu.VMEM((nc, rows, columns), bf16),
            pltpu.VMEM((nc, rows, columns), bf16),
            pltpu.SemaphoreType.DMA,
            dma(n), dma(n), dma(nc), dma(nc), dma(nc), dma(nc), dma(n_mp), dma(n_mp),
            dma(n_mp), dma(n_mp), dma(n), dma(n), dma(nc), dma(nc), dma(nc), dma(nc),
            pltpu.SemaphoreType.DMA,
        ],
        compiler_params=pltpu.CompilerParams(
            collective_id=0, has_side_effects=True, vmem_limit_bytes=VMEM_BYTES
        ),
    )(patches, embed, weight, counts)


def spread_kernel(n, n_mp, grads, squares, gathered, loss, zsq, psq, mine, ps, pr, fs, fr, zs, zr, cs, cr, loc_sem):
    d, m = lax.axis_index("dp"), lax.axis_index("mp")
    core, chip = lax.rem(d, 2), d // 2
    partner = d + 1 - 2 * core
    nc = n // 2
    greet(n, n_mp, d, m)

    def g_copy(i):
        return remote(grads, gathered.at[d], ps.at[i], pr.at[i], {"dp": 2 * lax.rem(chip + i, nc) + core})

    def g_own():
        return remote(grads, gathered.at[d], ps.at[0], pr.at[0], {"dp": partner})

    def f_copy(i):
        source = 2 * lax.rem(chip + nc - i, nc) + core
        return remote(gathered.at[source], gathered.at[source], fs.at[i], fr.at[i], {"dp": partner})

    def z_copy(i):
        return remote(squares, zsq.at[i], zs.at[i], zr.at[i], {"mp": lax.rem(m + i, n_mp)})

    def c_copy(i):
        return remote(mine, psq.at[i], cs.at[i], cr.at[i], {"dp": lax.rem(d + i, n)})

    for i in range(1, n_mp):
        z_copy(i).start()
    for i in range(1, nc):
        g_copy(i).start()
    g_own().start()
    own = pltpu.make_async_copy(grads, gathered.at[d], loc_sem)
    own.start()
    value = squares[...]
    for i in range(1, n_mp):
        z_copy(i).wait_recv()
        value = value + zsq[i]
    mine[...] = value
    for i in range(1, n):
        c_copy(i).start()
    for i in range(1, nc):
        g_copy(i).wait_recv()
        f_copy(i).start()
    for i in range(1, n):
        c_copy(i).wait_recv()
        value = value + psq[i]
    loss[...] = value
    g_own().wait()
    own.wait()
    for i in range(1, n_mp):
        z_copy(i).wait_send()
    for i in range(1, nc):
        g_copy(i).wait_send()
        f_copy(i).wait()
    for i in range(1, n):
        c_copy(i).wait_send()


def spread(grads, squares, n, n_mp):
    nc = n // 2
    dma = lambda k: pltpu.SemaphoreType.DMA((k,))
    vmem = pl.BlockSpec(memory_space=pltpu.VMEM)
    return pl.pallas_call(
        functools.partial(spread_kernel, n, n_mp),
        out_shape=(
            jax.ShapeDtypeStruct((n,) + grads.shape, grads.dtype),
            jax.ShapeDtypeStruct((8, 128), jnp.float32),
        ),
        in_specs=[vmem, vmem],
        out_specs=(vmem, vmem),
        scratch_shapes=[
            pltpu.VMEM((n_mp, 8, 128), jnp.float32),
            pltpu.VMEM((n, 8, 128), jnp.float32),
            pltpu.VMEM((8, 128), jnp.float32),
            dma(nc), dma(nc), dma(nc), dma(nc), dma(n_mp), dma(n_mp), dma(n), dma(n),
            pltpu.SemaphoreType.DMA,
        ],
        compiler_params=pltpu.CompilerParams(
            collective_id=1, has_side_effects=True, vmem_limit_bytes=VMEM_BYTES
        ),
    )(grads, squares)


def layer_norm(values):
    center = values - jnp.mean(values, axis=-1, keepdims=True)
    spread = jnp.mean(center * center, axis=-1, keepdims=True)
    return center * lax.rsqrt(spread + 1e-06)


def norm_grad(values, cotangent):
    return jax.vjp(layer_norm, values)[1](cotangent)[0]


def attend_block(query_raw, key_raw, value_rows, segment, target):
    inverse_root = 1.0 / math.sqrt(HD)
    query_normed = layer_norm(query_raw).astype(jnp.bfloat16)
    key_normed = layer_norm(key_raw).astype(jnp.bfloat16)
    scores = (
        jnp.einsum("qhd,khd->hqk", query_normed, key_normed, preferred_element_type=jnp.float32)
        * inverse_root
    )
    valid = segment >= 0
    allowed = (segment[:, None] == segment[None, :]) & valid[:, None]
    exponent = jnp.where(allowed[None], jnp.exp(scores), 0.0)
    denominator = jnp.sum(exponent, axis=-1, keepdims=True)
    denominator = jnp.where(valid[None, :, None], denominator, 1.0)
    weights = (exponent / denominator).astype(jnp.bfloat16)
    attended = jnp.einsum("hqk,khd->qhd", weights, value_rows, preferred_element_type=jnp.float32)
    feature_count = attended.shape[1] * attended.shape[2]
    error_rows = jnp.where(
        valid[:, None], attended.reshape(-1, feature_count) - target.astype(jnp.float32), 0.0
    )
    squared_sum = jnp.sum(error_rows * error_rows)
    return (query_normed, key_normed, weights, error_rows, squared_sum)


def attend_back(
    query_raw, key_raw, query_normed, key_normed, value_rows, weights, error_rows, patch_total
):
    inverse_root = 1.0 / math.sqrt(HD)
    out_grad = (error_rows / patch_total).astype(jnp.bfloat16).reshape(query_normed.shape)
    prob_grad = jnp.einsum("qhd,khd->hqk", out_grad, value_rows, preferred_element_type=jnp.float32)
    value_grad = jnp.einsum(
        "hqk,qhd->khd", weights, out_grad, preferred_element_type=jnp.float32
    ).astype(jnp.bfloat16)
    weight_float = weights.astype(jnp.float32)
    score_grad = (
        weight_float
        * (prob_grad - jnp.sum(prob_grad * weight_float, axis=-1, keepdims=True))
        * inverse_root
    ).astype(jnp.bfloat16)
    normed_grad_q = jnp.einsum(
        "hqk,khd->qhd", score_grad, key_normed, preferred_element_type=jnp.float32
    )
    normed_grad_k = jnp.einsum(
        "hqk,qhd->khd", score_grad, query_normed, preferred_element_type=jnp.float32
    )
    query_grad = norm_grad(query_raw, normed_grad_q).astype(jnp.bfloat16)
    key_grad = norm_grad(key_raw, normed_grad_k).astype(jnp.bfloat16)
    return jnp.stack([query_grad, key_grad, value_grad], axis=1)


def local(n, n_mp, patches, embed_weight, project_weight, patch_counts, segment_ids, targets):
    counts = jnp.broadcast_to(jnp.sum(patch_counts).astype(jnp.float32), (8, 128))
    row_total = patches.shape[0]
    normed, projected, total = project(
        patches, embed_weight, jnp.transpose(project_weight, (1, 0, 2)), counts, n, n_mp
    )
    patch_total = total[0, 0]
    head_dev = project_weight.shape[2] // HD
    projected = projected.reshape(row_total, 3, head_dev, HD)
    query_raw = projected[:, 0]
    key_raw = projected[:, 1]
    value_rows = projected[:, 2].astype(jnp.bfloat16)
    query_normed, key_normed, weights, error_rows, squared_sum = attend_block(
        query_raw, key_raw, value_rows, segment_ids, targets
    )
    grad_rows = attend_back(
        query_raw, key_raw, query_normed, key_normed, value_rows, weights, error_rows, patch_total
    )
    gathered, squares = spread(
        grad_rows.reshape(row_total, -1), jnp.broadcast_to(squared_sum, (8, 128)), n, n_mp
    )
    loss_value = squares[0, 0] / (2.0 * patch_total)
    weight_grad = lax.dot_general(
        normed.reshape(-1, normed.shape[2]),
        gathered.reshape(-1, gathered.shape[2]),
        (((0,), (0,)), ((), ())),
        preferred_element_type=jnp.float32,
    )
    return (weight_grad.reshape(weight_grad.shape[0], 3, -1), loss_value)


def solution(mesh):
    in_specs = (
        P("dp", None),
        P(("mp", "dp"), None),
        P("dp", None, "mp"),
        P("dp"),
        P("dp"),
        P("dp", "mp"),
    )
    out_specs = (P("dp", None, "mp"), P())
    return jax.shard_map(
        functools.partial(local, mesh.shape["dp"], mesh.shape["mp"]), mesh=mesh, in_specs=in_specs, out_specs=out_specs, check_vma=False)
```

```python
import functools
import math

import jax
import jax.numpy as jnp
from jax import lax
from jax.experimental import pallas as pl
from jax.experimental.pallas import tpu as pltpu
from jax.sharding import PartitionSpec as P

HD = 128
MESH = pl.DeviceIdType.MESH
VMEM_BYTES = 62 * 1024 * 1024


def remote(src, dst, send_sem, recv_sem, device_id):
    return pltpu.make_async_remote_copy(
        src_ref=src, dst_ref=dst, send_sem=send_sem, recv_sem=recv_sem,
        device_id=device_id, device_id_type=MESH,
    )


def greet(n, n_mp, d, m):
    barrier = pltpu.get_barrier_semaphore()
    for i in range(1, n):
        pl.semaphore_signal(barrier, inc=1, device_id={"dp": lax.rem(d + i, n)}, device_id_type=MESH)
    for i in range(1, n_mp):
        pl.semaphore_signal(barrier, inc=1, device_id={"mp": lax.rem(m + i, n_mp)}, device_id_type=MESH)
    pl.semaphore_wait(barrier, n - 1 + n_mp - 1)


def project_kernel(
    n, n_mp,
    patches, embed, weight_hbm, counts,
    normed, raw, total,
    pall, zbuf, eblk, wbuf, stats, cbuf, pbuf, pin, sbuf, rbuf,
    w_sem, cs, cr, ps, pr, fs, fr, zs, zr, es, er, ss, sr, bs, br, qs, qr, loc_sem,
):
    d, m = lax.axis_index("dp"), lax.axis_index("mp")
    core, chip = lax.rem(d, 2), d // 2
    partner = d + 1 - 2 * core
    nc, per = n // 2, n // n_mp
    rows = patches.shape[0]
    tile = weight_hbm.shape[2]

    load = pltpu.make_async_copy(weight_hbm, wbuf, w_sem)
    load.start()
    greet(n, n_mp, d, m)

    def peer(i):
        return 2 * lax.rem(chip + i, nc) + core

    def source(i):
        return 2 * lax.rem(chip + nc - i, nc) + core

    def far(i):
        return lax.rem(d + i, n)

    def z_copy(i):
        return remote(embed, zbuf.at[i], zs.at[i], zr.at[i], {"mp": lax.rem(m + i, n_mp)})

    for i in range(1, n_mp):
        z_copy(i).start()

    def c_copy(i):
        return remote(counts, cbuf.at[i], cs.at[i], cr.at[i], {"dp": far(i)})

    def p_copy(i):
        return remote(patches, pall.at[d], ps.at[i], pr.at[i], {"dp": peer(i)})

    def p_own():
        return remote(patches, pall.at[d], ps.at[0], pr.at[0], {"dp": partner})

    def f_copy(i):
        return remote(pall.at[source(i)], pall.at[source(i)], fs.at[i], fr.at[i], {"dp": partner})

    def e_target(i):
        return lax.rem(m + n_mp - i, n_mp) * per + d // n_mp

    def e_copy(i, src):
        return remote(src, eblk.at[lax.rem(d, n_mp)], es.at[i], er.at[lax.rem(d, n_mp)], {"dp": e_target(i)})

    def e_local(i, src):
        return pltpu.make_async_copy(src, eblk.at[lax.rem(d, n_mp)], loc_sem)

    def e_start(i, src):
        @pl.when(e_target(i) != d)
        def _():
            e_copy(i, src).start()

        @pl.when(e_target(i) == d)
        def _():
            e_local(i, src).start()
            e_local(i, src).wait()

    p_own().start()
    for i in range(1, nc):
        p_copy(i).start()
    for i in range(1, n):
        c_copy(i).start()
    e_start(0, embed)
    pall[d] = patches[...]
    for i in range(1, nc):
        p_copy(i).wait_recv()
        f_copy(i).start()
    for i in range(1, n_mp):
        z_copy(i).wait_recv()
        e_start(i, zbuf.at[i])
    sum_counts = counts[...]
    for i in range(1, n):
        c_copy(i).wait_recv()
        sum_counts = sum_counts + cbuf[i]
    total[...] = sum_counts
    p_own().wait_recv()
    for i in range(1, nc):
        f_copy(i).wait_recv()
    for q in range(n_mp):
        origin = lax.rem(d, per) * n_mp + q

        @pl.when(origin != d)
        def _():
            remote(eblk.at[q], eblk.at[q], es.at[q], er.at[q], {"dp": partner}).wait_recv()

    width = eblk.shape[0] * eblk.shape[1]
    feature_total = width * n
    lane = lax.broadcasted_iota(jnp.int32, (rows, 128), 1)

    def embed_block(b, carry):
        block = pall[b]
        parts = jnp.concatenate(
            [eblk[q] for q in range(n_mp)], axis=0
        )
        value = lax.dot_general(
            block, parts, (((1,), (1,)), ((), ())), preferred_element_type=jnp.float32
        ).astype(jnp.bfloat16)
        normed[b] = value
        value = value.astype(jnp.float32)
        mean = jnp.sum(value, axis=-1, keepdims=True) * (1.0 / width)
        center = value - mean
        square = jnp.sum(center * center, axis=-1, keepdims=True)
        both = jnp.where(lane == 0, mean, jnp.where(lane == 1, square, 0.0))
        stats[0, b] = both.T[:8]
        return carry

    lax.fori_loop(0, n, embed_block, 0)

    def s_copy(i):
        return remote(stats.at[0], stats.at[i], ss.at[i], sr.at[i], {"dp": far(i)})

    for i in range(1, n):
        s_copy(i).start()
    for i in range(1, n):
        s_copy(i).wait_recv()

    load.wait()

    def norm_block(b, carry):
        mean = stats[0, b, 0:1, :]
        for i in range(1, n):
            mean = mean + stats[i, b, 0:1, :]
        mean = mean * (1.0 / n)
        square = jnp.zeros_like(mean)
        for i in range(n):
            gap = stats[i, b, 0:1, :] - mean
            square = square + stats[i, b, 1:2, :] + width * (gap * gap)
        scale = lax.rsqrt(square * (1.0 / feature_total) + 1e-06)
        row = lax.broadcasted_iota(jnp.int32, (128, rows), 0)
        both = jnp.where(row == 0, mean, jnp.where(row == 1, scale, 0.0)).T
        value = normed[b].astype(jnp.float32)
        normed[b] = ((value - both[:, 0:1]) * both[:, 1:2]).astype(jnp.bfloat16)
        return carry

    lax.fori_loop(0, n, norm_block, 0)

    def b_copy(i):
        return remote(pbuf.at[i], pin.at[i], bs.at[i], br.at[i], {"dp": partner})

    def q_copy(i):
        return remote(sbuf.at[i], rbuf.at[i], qs.at[i], qr.at[i], {"dp": peer(i)})

    def other_part(k, carry):
        i = lax.rem(k + 1, nc)
        block = normed[2 * lax.rem(chip + i, nc) + 1 - core]
        for s in range(3):
            pbuf[i, :, s * tile:(s + 1) * tile] = jnp.dot(
                block, wbuf[s], preferred_element_type=jnp.float32
            ).astype(jnp.bfloat16)
        b_copy(i).start()
        return carry

    lax.fori_loop(0, nc, other_part, 0)

    def own_part(i, carry):
        block = normed[peer(i)]
        b_copy(i).wait_recv()
        for s in range(3):
            cols = slice(s * tile, (s + 1) * tile)
            sbuf[i, :, cols] = (
                jnp.dot(block, wbuf[s], preferred_element_type=jnp.float32)
                + pin[i, :, cols].astype(jnp.float32)
            ).astype(jnp.bfloat16)
        q_copy(i).start()
        return carry

    lax.fori_loop(1, nc, own_part, 0)
    block = normed[d]
    b_copy(0).wait_recv()
    for s in range(3):
        cols = slice(s * tile, (s + 1) * tile)
        raw[:, cols] = jnp.dot(block, wbuf[s], preferred_element_type=jnp.float32) + pin[
            0, :, cols
        ].astype(jnp.float32)

    def take(i, carry):
        q_copy(i).wait_recv()
        raw[...] += rbuf[i].astype(jnp.float32)
        return carry

    lax.fori_loop(1, nc, take, 0)

    p_own().wait_send()
    for i in range(1, n_mp):
        z_copy(i).wait_send()
    for i in range(n_mp):
        @pl.when(e_target(i) != d)
        def _():
            e_copy(i, embed).wait_send()
    for i in range(1, nc):
        p_copy(i).wait_send()
        f_copy(i).wait_send()
        q_copy(i).wait_send()
    for i in range(nc):
        b_copy(i).wait_send()
    for i in range(1, n):
        c_copy(i).wait_send()
        s_copy(i).wait_send()


def project(patches, embed, weight, counts, n, n_mp):
    rows, width = patches.shape
    pieces = embed.shape[0]
    features, columns = weight.shape[1], 3 * weight.shape[2]
    nc = n // 2
    dma = lambda k: pltpu.SemaphoreType.DMA((k,))
    vmem = pl.BlockSpec(memory_space=pltpu.VMEM)
    bf16, f32 = jnp.bfloat16, jnp.float32
    return pl.pallas_call(
        functools.partial(project_kernel, n, n_mp),
        out_shape=(
            jax.ShapeDtypeStruct((n, rows, features), bf16),
            jax.ShapeDtypeStruct((rows, columns), f32),
            jax.ShapeDtypeStruct((8, 128), f32),
        ),
        in_specs=[vmem, vmem, pl.BlockSpec(memory_space=pl.ANY), vmem],
        out_specs=(vmem, vmem, vmem),
        scratch_shapes=[
            pltpu.VMEM((n, rows, width), bf16),
            pltpu.VMEM((n_mp, pieces, width), bf16),
            pltpu.VMEM((n_mp, pieces, width), bf16),
            pltpu.VMEM(weight.shape, bf16),
            pltpu.VMEM((n, n, 8, rows), f32),
            pltpu.VMEM((n, 8, 128), f32),
            pltpu.VMEM((nc, rows, columns), bf16),
            pltpu.VMEM((nc, rows, columns), bf16),
            pltpu.VMEM((nc, rows, columns), bf16),
            pltpu.VMEM((nc, rows, columns), bf16),
            pltpu.SemaphoreType.DMA,
            dma(n), dma(n), dma(nc), dma(nc), dma(nc), dma(nc), dma(n_mp), dma(n_mp),
            dma(n_mp), dma(n_mp), dma(n), dma(n), dma(nc), dma(nc), dma(nc), dma(nc),
            pltpu.SemaphoreType.DMA,
        ],
        compiler_params=pltpu.CompilerParams(
            collective_id=0, has_side_effects=True, vmem_limit_bytes=VMEM_BYTES
        ),
    )(patches, embed, weight, counts)


def grid_side(nc):
    side = math.isqrt(nc)
    assert side * side == nc
    return side


def chip_at(chip, side, h, i, j):
    a, b = chip // side, lax.rem(chip, side)
    da, db = (j, i) if h == 0 else (i, j)
    return lax.rem(a + da + side, side) * side + lax.rem(b + db + side, side)


def spread_kernel(n, n_mp, chunks, grads, squares, gathered, loss, zsq, psq, mine, ps, pr, gs, gr, fs, fr, zs, zr, cs, cr, loc_sem):
    d, m = lax.axis_index("dp"), lax.axis_index("mp")
    core, chip = lax.rem(d, 2), d // 2
    partner = d + 1 - 2 * core
    nc = n // 2
    side = grid_side(nc)
    span = grads.shape[0] // chunks
    greet(n, n_mp, d, m)

    def part(k):
        return pl.ds(k * span, span)

    def block(k, i, j):
        if i == 0 and j == 0:
            return grads.at[part(k)]
        return gathered.at[2 * chip_at(chip, side, k % 2, -i, -j) + core, part(k)]

    def landing(k, i, j):
        return gathered.at[2 * chip_at(chip, side, k % 2, -i, -j) + core, part(k)]

    def first(k, i):
        to = 2 * chip_at(chip, side, k % 2, i, 0) + core
        return remote(block(k, 0, 0), landing(k, 0, 0), ps.at[k, i], pr.at[k, i], {"dp": to})

    def second(k, i, j):
        to = 2 * chip_at(chip, side, k % 2, 0, j) + core
        return remote(block(k, i, 0), landing(k, i, 0), gs.at[k, i, j], gr.at[k, i, j], {"dp": to})

    def across(k, i, j):
        return remote(block(k, i, j), landing(k, i, j), fs.at[k, i, j], fr.at[k, i, j], {"dp": partner})

    def z_copy(i):
        return remote(squares, zsq.at[i], zs.at[i], zr.at[i], {"mp": lax.rem(m + i, n_mp)})

    def c_copy(i):
        return remote(mine, psq.at[i], cs.at[i], cr.at[i], {"dp": lax.rem(d + i, n)})

    for i in range(1, n_mp):
        z_copy(i).start()
    for k in range(chunks):
        for i in range(1, side):
            first(k, i).start()
    for k in range(chunks):
        for j in range(1, side):
            second(k, 0, j).start()
        across(k, 0, 0).start()
    own = pltpu.make_async_copy(grads, gathered.at[d], loc_sem)
    own.start()
    value = squares[...]
    for i in range(1, n_mp):
        z_copy(i).wait_recv()
        value = value + zsq[i]
    mine[...] = value
    for i in range(1, n):
        c_copy(i).start()
    for k in range(chunks):
        for i in range(1, side):
            first(k, i).wait_recv()
            for j in range(1, side):
                second(k, i, j).start()
            across(k, i, 0).start()
    for i in range(1, n):
        c_copy(i).wait_recv()
        value = value + psq[i]
    loss[...] = value
    for i in range(side):
        for k in range(chunks):
            for j in range(1, side):
                second(k, i, j).wait_recv()
                across(k, i, j).start()
    own.wait()
    for k in range(chunks):
        for i in range(side):
            if i:
                first(k, i).wait_send()
            for j in range(side):
                if j:
                    second(k, i, j).wait_send()
                across(k, i, j).wait()
    for i in range(1, n_mp):
        z_copy(i).wait_send()
    for i in range(1, n):
        c_copy(i).wait_send()


def spread(grads, squares, n, n_mp):
    chunks = 4
    side = grid_side(n // 2)
    dma = lambda *k: pltpu.SemaphoreType.DMA(k)
    vmem = pl.BlockSpec(memory_space=pltpu.VMEM)
    return pl.pallas_call(
        functools.partial(spread_kernel, n, n_mp, chunks),
        out_shape=(
            jax.ShapeDtypeStruct((n,) + grads.shape, grads.dtype),
            jax.ShapeDtypeStruct((8, 128), jnp.float32),
        ),
        in_specs=[vmem, vmem],
        out_specs=(vmem, vmem),
        scratch_shapes=[
            pltpu.VMEM((n_mp, 8, 128), jnp.float32),
            pltpu.VMEM((n, 8, 128), jnp.float32),
            pltpu.VMEM((8, 128), jnp.float32),
            dma(chunks, side), dma(chunks, side),
            dma(chunks, side, side), dma(chunks, side, side),
            dma(chunks, side, side), dma(chunks, side, side),
            dma(n_mp), dma(n_mp), dma(n), dma(n),
            pltpu.SemaphoreType.DMA,
        ],
        compiler_params=pltpu.CompilerParams(
            collective_id=1, has_side_effects=True, vmem_limit_bytes=VMEM_BYTES
        ),
    )(grads, squares)


def weight_grad_kernel(left, right, out):
    out[0] = lax.dot_general(
        left[...], right[...], (((0,), (0,)), ((), ())), preferred_element_type=jnp.float32
    )


def weight_grad_of(normed, grads):
    rows, features = normed.shape
    tile = grads.shape[1] // 3
    width = 256 if features % 256 == 0 else features
    return pl.pallas_call(
        weight_grad_kernel,
        grid=(3, features // width),
        out_shape=jax.ShapeDtypeStruct((3, features, tile), jnp.float32),
        in_specs=[
            pl.BlockSpec((rows, width), lambda s, f: (0, f)),
            pl.BlockSpec((rows, tile), lambda s, f: (0, s)),
        ],
        out_specs=pl.BlockSpec((1, width, tile), lambda s, f: (s, f, 0)),
    )(normed, grads)


def layer_norm(values):
    center = values - jnp.mean(values, axis=-1, keepdims=True)
    spread = jnp.mean(center * center, axis=-1, keepdims=True)
    return center * lax.rsqrt(spread + 1e-06)


def norm_grad(values, cotangent):
    return jax.vjp(layer_norm, values)[1](cotangent)[0]


def attend_block(query_raw, key_raw, value_rows, segment, target):
    inverse_root = 1.0 / math.sqrt(HD)
    query_normed = layer_norm(query_raw).astype(jnp.bfloat16)
    key_normed = layer_norm(key_raw).astype(jnp.bfloat16)
    scores = (
        jnp.einsum("qhd,khd->hqk", query_normed, key_normed, preferred_element_type=jnp.float32)
        * inverse_root
    )
    valid = segment >= 0
    allowed = (segment[:, None] == segment[None, :]) & valid[:, None]
    exponent = jnp.where(allowed[None], jnp.exp(scores), 0.0)
    denominator = jnp.sum(exponent, axis=-1, keepdims=True)
    denominator = jnp.where(valid[None, :, None], denominator, 1.0)
    weights = (exponent / denominator).astype(jnp.bfloat16)
    attended = jnp.einsum("hqk,khd->qhd", weights, value_rows, preferred_element_type=jnp.float32)
    feature_count = attended.shape[1] * attended.shape[2]
    error_rows = jnp.where(
        valid[:, None], attended.reshape(-1, feature_count) - target.astype(jnp.float32), 0.0
    )
    squared_sum = jnp.sum(error_rows * error_rows)
    return (query_normed, key_normed, weights, error_rows, squared_sum)


def attend_back(
    query_raw, key_raw, query_normed, key_normed, value_rows, weights, error_rows, patch_total
):
    inverse_root = 1.0 / math.sqrt(HD)
    out_grad = (error_rows / patch_total).astype(jnp.bfloat16).reshape(query_normed.shape)
    prob_grad = jnp.einsum("qhd,khd->hqk", out_grad, value_rows, preferred_element_type=jnp.float32)
    value_grad = jnp.einsum(
        "hqk,qhd->khd", weights, out_grad, preferred_element_type=jnp.float32
    ).astype(jnp.bfloat16)
    weight_float = weights.astype(jnp.float32)
    score_grad = (
        weight_float
        * (prob_grad - jnp.sum(prob_grad * weight_float, axis=-1, keepdims=True))
        * inverse_root
    ).astype(jnp.bfloat16)
    normed_grad_q = jnp.einsum(
        "hqk,khd->qhd", score_grad, key_normed, preferred_element_type=jnp.float32
    )
    normed_grad_k = jnp.einsum(
        "hqk,qhd->khd", score_grad, query_normed, preferred_element_type=jnp.float32
    )
    query_grad = norm_grad(query_raw, normed_grad_q).astype(jnp.bfloat16)
    key_grad = norm_grad(key_raw, normed_grad_k).astype(jnp.bfloat16)
    return jnp.stack([query_grad, key_grad, value_grad], axis=1)


def local(n, n_mp, patches, embed_weight, project_weight, patch_counts, segment_ids, targets):
    counts = jnp.broadcast_to(jnp.sum(patch_counts).astype(jnp.float32), (8, 128))
    row_total = patches.shape[0]
    normed, projected, total = project(
        patches, embed_weight, jnp.transpose(project_weight, (1, 0, 2)), counts, n, n_mp
    )
    patch_total = total[0, 0]
    head_dev = project_weight.shape[2] // HD
    projected = projected.reshape(row_total, 3, head_dev, HD)
    query_raw = projected[:, 0]
    key_raw = projected[:, 1]
    value_rows = projected[:, 2].astype(jnp.bfloat16)
    query_normed, key_normed, weights, error_rows, squared_sum = attend_block(
        query_raw, key_raw, value_rows, segment_ids, targets
    )
    grad_rows = attend_back(
        query_raw, key_raw, query_normed, key_normed, value_rows, weights, error_rows, patch_total
    )
    gathered, squares = spread(
        grad_rows.reshape(row_total, -1), jnp.broadcast_to(squared_sum, (8, 128)), n, n_mp
    )
    loss_value = squares[0, 0] / (2.0 * patch_total)
    weight_grad = weight_grad_of(
        normed.reshape(-1, normed.shape[2]), gathered.reshape(-1, gathered.shape[2])
    )
    return (jnp.transpose(weight_grad, (1, 0, 2)), loss_value)


def solution(mesh):
    in_specs = (
        P("dp", None),
        P(("mp", "dp"), None),
        P("dp", None, "mp"),
        P("dp"),
        P("dp"),
        P("dp", "mp"),
    )
    out_specs = (P("dp", None, "mp"), P())
    return jax.shard_map(
        functools.partial(local, mesh.shape["dp"], mesh.shape["mp"]), mesh=mesh, in_specs=in_specs, out_specs=out_specs, check_vma=False)
```

```python
import functools
import math

import jax
import jax.numpy as jnp
from jax import lax
from jax.experimental import pallas as pl
from jax.experimental.pallas import tpu as pltpu
from jax.sharding import PartitionSpec as P

HD = 128
MESH = pl.DeviceIdType.MESH
VMEM_BYTES = 62 * 1024 * 1024


def remote(src, dst, send_sem, recv_sem, device_id):
    return pltpu.make_async_remote_copy(
        src_ref=src, dst_ref=dst, send_sem=send_sem, recv_sem=recv_sem,
        device_id=device_id, device_id_type=MESH,
    )


def greet(n, n_mp, d, m):
    barrier = pltpu.get_barrier_semaphore()
    for i in range(1, n):
        pl.semaphore_signal(barrier, inc=1, device_id={"dp": lax.rem(d + i, n)}, device_id_type=MESH)
    for i in range(1, n_mp):
        pl.semaphore_signal(barrier, inc=1, device_id={"mp": lax.rem(m + i, n_mp)}, device_id_type=MESH)
    pl.semaphore_wait(barrier, n - 1 + n_mp - 1)


def project_kernel(
    n, n_mp,
    patches, embed, weight_hbm, counts,
    normed_t, raw, total,
    normed, pall, zbuf, eblk, wbuf, stats, cbuf, pbuf, pin, sbuf, rbuf,
    w_sem, cs, cr, ps, pr, fs, fr, zs, zr, es, er, ss, sr, bs, br, qs, qr, loc_sem,
):
    d, m = lax.axis_index("dp"), lax.axis_index("mp")
    core, chip = lax.rem(d, 2), d // 2
    partner = d + 1 - 2 * core
    nc, per = n // 2, n // n_mp
    rows = patches.shape[0]
    tile = weight_hbm.shape[2]

    load = pltpu.make_async_copy(weight_hbm, wbuf, w_sem)
    load.start()
    greet(n, n_mp, d, m)

    def peer(i):
        return 2 * lax.rem(chip + i, nc) + core

    def source(i):
        return 2 * lax.rem(chip + nc - i, nc) + core

    def far(i):
        return lax.rem(d + i, n)

    def z_copy(i):
        return remote(embed, zbuf.at[i], zs.at[i], zr.at[i], {"mp": lax.rem(m + i, n_mp)})

    for i in range(1, n_mp):
        z_copy(i).start()

    def c_copy(i):
        return remote(counts, cbuf.at[i], cs.at[i], cr.at[i], {"dp": far(i)})

    def p_copy(i):
        return remote(patches, pall.at[d], ps.at[i], pr.at[i], {"dp": peer(i)})

    def p_own():
        return remote(patches, pall.at[d], ps.at[0], pr.at[0], {"dp": partner})

    def f_copy(i):
        return remote(pall.at[source(i)], pall.at[source(i)], fs.at[i], fr.at[i], {"dp": partner})

    def e_target(i):
        return lax.rem(m + n_mp - i, n_mp) * per + d // n_mp

    def e_copy(i, src):
        return remote(src, eblk.at[lax.rem(d, n_mp)], es.at[i], er.at[lax.rem(d, n_mp)], {"dp": e_target(i)})

    def e_local(i, src):
        return pltpu.make_async_copy(src, eblk.at[lax.rem(d, n_mp)], loc_sem)

    def e_start(i, src):
        @pl.when(e_target(i) != d)
        def _():
            e_copy(i, src).start()

        @pl.when(e_target(i) == d)
        def _():
            e_local(i, src).start()
            e_local(i, src).wait()

    p_own().start()
    for i in range(1, nc):
        p_copy(i).start()
    for i in range(1, n):
        c_copy(i).start()
    e_start(0, embed)
    pall[d] = patches[...]
    for i in range(1, nc):
        p_copy(i).wait_recv()
        f_copy(i).start()
    for i in range(1, n_mp):
        z_copy(i).wait_recv()
        e_start(i, zbuf.at[i])
    sum_counts = counts[...]
    for i in range(1, n):
        c_copy(i).wait_recv()
        sum_counts = sum_counts + cbuf[i]
    total[...] = sum_counts
    p_own().wait_recv()
    for i in range(1, nc):
        f_copy(i).wait_recv()
    for q in range(n_mp):
        origin = lax.rem(d, per) * n_mp + q

        @pl.when(origin != d)
        def _():
            remote(eblk.at[q], eblk.at[q], es.at[q], er.at[q], {"dp": partner}).wait_recv()

    width = eblk.shape[0] * eblk.shape[1]
    feature_total = width * n
    lane = lax.broadcasted_iota(jnp.int32, (rows, 128), 1)

    def embed_block(b, carry):
        block = pall[b]
        parts = jnp.concatenate(
            [eblk[q] for q in range(n_mp)], axis=0
        )
        value = lax.dot_general(
            block, parts, (((1,), (1,)), ((), ())), preferred_element_type=jnp.float32
        ).astype(jnp.bfloat16)
        normed[b] = value
        value = value.astype(jnp.float32)
        mean = jnp.sum(value, axis=-1, keepdims=True) * (1.0 / width)
        center = value - mean
        square = jnp.sum(center * center, axis=-1, keepdims=True)
        both = jnp.where(lane == 0, mean, jnp.where(lane == 1, square, 0.0))
        stats[0, b] = both.T[:8]
        return carry

    lax.fori_loop(0, n, embed_block, 0)

    def s_copy(i):
        return remote(stats.at[0], stats.at[i], ss.at[i], sr.at[i], {"dp": far(i)})

    for i in range(1, n):
        s_copy(i).start()
    for i in range(1, n):
        s_copy(i).wait_recv()

    load.wait()

    def norm_block(b, carry):
        mean = stats[0, b, 0:1, :]
        for i in range(1, n):
            mean = mean + stats[i, b, 0:1, :]
        mean = mean * (1.0 / n)
        square = jnp.zeros_like(mean)
        for i in range(n):
            gap = stats[i, b, 0:1, :] - mean
            square = square + stats[i, b, 1:2, :] + width * (gap * gap)
        scale = lax.rsqrt(square * (1.0 / feature_total) + 1e-06)
        row = lax.broadcasted_iota(jnp.int32, (128, rows), 0)
        both = jnp.where(row == 0, mean, jnp.where(row == 1, scale, 0.0)).T
        value = normed[b].astype(jnp.float32)
        normed[b] = ((value - both[:, 0:1]) * both[:, 1:2]).astype(jnp.bfloat16)
        return carry

    lax.fori_loop(0, n, norm_block, 0)

    def b_copy(i):
        return remote(pbuf.at[i], pin.at[i], bs.at[i], br.at[i], {"dp": partner})

    def q_copy(i):
        return remote(sbuf.at[i], rbuf.at[i], qs.at[i], qr.at[i], {"dp": peer(i)})

    def other_part(k, carry):
        i = lax.rem(k + 1, nc)
        block = normed[2 * lax.rem(chip + i, nc) + 1 - core]
        for s in range(3):
            pbuf[i, :, s * tile:(s + 1) * tile] = jnp.dot(
                block, wbuf[s], preferred_element_type=jnp.float32
            ).astype(jnp.bfloat16)
        b_copy(i).start()
        return carry

    lax.fori_loop(0, nc, other_part, 0)

    def own_part(i, carry):
        block = normed[peer(i)]
        b_copy(i).wait_recv()
        for s in range(3):
            cols = slice(s * tile, (s + 1) * tile)
            sbuf[i, :, cols] = (
                jnp.dot(block, wbuf[s], preferred_element_type=jnp.float32)
                + pin[i, :, cols].astype(jnp.float32)
            ).astype(jnp.bfloat16)
        q_copy(i).start()
        return carry

    lax.fori_loop(1, nc, own_part, 0)
    block = normed[d]
    b_copy(0).wait_recv()
    for s in range(3):
        cols = slice(s * tile, (s + 1) * tile)
        raw[:, cols] = jnp.dot(block, wbuf[s], preferred_element_type=jnp.float32) + pin[
            0, :, cols
        ].astype(jnp.float32)

    for b in range(n):
        normed_t[:, b * rows:(b + 1) * rows] = normed[b].T

    def take(i, carry):
        q_copy(i).wait_recv()
        raw[...] += rbuf[i].astype(jnp.float32)
        return carry

    lax.fori_loop(1, nc, take, 0)

    p_own().wait_send()
    for i in range(1, n_mp):
        z_copy(i).wait_send()
    for i in range(n_mp):
        @pl.when(e_target(i) != d)
        def _():
            e_copy(i, embed).wait_send()
    for i in range(1, nc):
        p_copy(i).wait_send()
        f_copy(i).wait_send()
        q_copy(i).wait_send()
    for i in range(nc):
        b_copy(i).wait_send()
    for i in range(1, n):
        c_copy(i).wait_send()
        s_copy(i).wait_send()


def project(patches, embed, weight, counts, n, n_mp):
    rows, width = patches.shape
    pieces = embed.shape[0]
    features, columns = weight.shape[1], 3 * weight.shape[2]
    nc = n // 2
    dma = lambda k: pltpu.SemaphoreType.DMA((k,))
    vmem = pl.BlockSpec(memory_space=pltpu.VMEM)
    bf16, f32 = jnp.bfloat16, jnp.float32
    return pl.pallas_call(
        functools.partial(project_kernel, n, n_mp),
        out_shape=(
            jax.ShapeDtypeStruct((features, n * rows), bf16),
            jax.ShapeDtypeStruct((rows, columns), f32),
            jax.ShapeDtypeStruct((8, 128), f32),
        ),
        in_specs=[vmem, vmem, pl.BlockSpec(memory_space=pl.ANY), vmem],
        out_specs=(vmem, vmem, vmem),
        scratch_shapes=[
            pltpu.VMEM((n, rows, features), bf16),
            pltpu.VMEM((n, rows, width), bf16),
            pltpu.VMEM((n_mp, pieces, width), bf16),
            pltpu.VMEM((n_mp, pieces, width), bf16),
            pltpu.VMEM(weight.shape, bf16),
            pltpu.VMEM((n, n, 8, rows), f32),
            pltpu.VMEM((n, 8, 128), f32),
            pltpu.VMEM((nc, rows, columns), bf16),
            pltpu.VMEM((nc, rows, columns), bf16),
            pltpu.VMEM((nc, rows, columns), bf16),
            pltpu.VMEM((nc, rows, columns), bf16),
            pltpu.SemaphoreType.DMA,
            dma(n), dma(n), dma(nc), dma(nc), dma(nc), dma(nc), dma(n_mp), dma(n_mp),
            dma(n_mp), dma(n_mp), dma(n), dma(n), dma(nc), dma(nc), dma(nc), dma(nc),
            pltpu.SemaphoreType.DMA,
        ],
        compiler_params=pltpu.CompilerParams(
            collective_id=0, has_side_effects=True, vmem_limit_bytes=VMEM_BYTES
        ),
    )(patches, embed, weight, counts)


def grid_side(nc):
    side = math.isqrt(nc)
    assert side * side == nc
    return side


def chip_at(chip, side, h, i, j):
    a, b = chip // side, lax.rem(chip, side)
    da, db = (j, i) if h == 0 else (i, j)
    return lax.rem(a + da + side, side) * side + lax.rem(b + db + side, side)


def spread_kernel(n, n_mp, chunks, grads, squares, gathered, loss, zsq, psq, mine, ps, pr, gs, gr, fs, fr, zs, zr, cs, cr, loc_sem):
    d, m = lax.axis_index("dp"), lax.axis_index("mp")
    core, chip = lax.rem(d, 2), d // 2
    partner = d + 1 - 2 * core
    nc = n // 2
    side = grid_side(nc)
    span = grads.shape[0] // chunks
    greet(n, n_mp, d, m)

    def part(k):
        return pl.ds(k * span, span)

    def block(k, i, j):
        if i == 0 and j == 0:
            return grads.at[part(k)]
        return gathered.at[2 * chip_at(chip, side, k % 2, -i, -j) + core, part(k)]

    def landing(k, i, j):
        return gathered.at[2 * chip_at(chip, side, k % 2, -i, -j) + core, part(k)]

    def first(k, i):
        to = 2 * chip_at(chip, side, k % 2, i, 0) + core
        return remote(block(k, 0, 0), landing(k, 0, 0), ps.at[k, i], pr.at[k, i], {"dp": to})

    def second(k, i, j):
        to = 2 * chip_at(chip, side, k % 2, 0, j) + core
        return remote(block(k, i, 0), landing(k, i, 0), gs.at[k, i, j], gr.at[k, i, j], {"dp": to})

    def across(k, i, j):
        return remote(block(k, i, j), landing(k, i, j), fs.at[k, i, j], fr.at[k, i, j], {"dp": partner})

    def z_copy(i):
        return remote(squares, zsq.at[i], zs.at[i], zr.at[i], {"mp": lax.rem(m + i, n_mp)})

    def c_copy(i):
        return remote(mine, psq.at[i], cs.at[i], cr.at[i], {"dp": lax.rem(d + i, n)})

    for i in range(1, n_mp):
        z_copy(i).start()
    for k in range(chunks):
        for i in range(1, side):
            first(k, i).start()
    for k in range(chunks):
        for j in range(1, side):
            second(k, 0, j).start()
        across(k, 0, 0).start()
    own = pltpu.make_async_copy(grads, gathered.at[d], loc_sem)
    own.start()
    value = squares[...]
    for i in range(1, n_mp):
        z_copy(i).wait_recv()
        value = value + zsq[i]
    mine[...] = value
    for i in range(1, n):
        c_copy(i).start()
    for k in range(chunks):
        for i in range(1, side):
            first(k, i).wait_recv()
            for j in range(1, side):
                second(k, i, j).start()
            across(k, i, 0).start()
    for i in range(1, n):
        c_copy(i).wait_recv()
        value = value + psq[i]
    loss[...] = value
    for i in range(side):
        for k in range(chunks):
            for j in range(1, side):
                second(k, i, j).wait_recv()
                across(k, i, j).start()
    own.wait()
    for k in range(chunks):
        for i in range(side):
            if i:
                first(k, i).wait_send()
            for j in range(side):
                if j:
                    second(k, i, j).wait_send()
                across(k, i, j).wait()
    for i in range(1, n_mp):
        z_copy(i).wait_send()
    for i in range(1, n):
        c_copy(i).wait_send()


def spread(grads, squares, n, n_mp):
    chunks = 4
    side = grid_side(n // 2)
    dma = lambda *k: pltpu.SemaphoreType.DMA(k)
    vmem = pl.BlockSpec(memory_space=pltpu.VMEM)
    return pl.pallas_call(
        functools.partial(spread_kernel, n, n_mp, chunks),
        out_shape=(
            jax.ShapeDtypeStruct((n,) + grads.shape, grads.dtype),
            jax.ShapeDtypeStruct((8, 128), jnp.float32),
        ),
        in_specs=[vmem, vmem],
        out_specs=(vmem, vmem),
        scratch_shapes=[
            pltpu.VMEM((n_mp, 8, 128), jnp.float32),
            pltpu.VMEM((n, 8, 128), jnp.float32),
            pltpu.VMEM((8, 128), jnp.float32),
            dma(chunks, side), dma(chunks, side),
            dma(chunks, side, side), dma(chunks, side, side),
            dma(chunks, side, side), dma(chunks, side, side),
            dma(n_mp), dma(n_mp), dma(n), dma(n),
            pltpu.SemaphoreType.DMA,
        ],
        compiler_params=pltpu.CompilerParams(
            collective_id=1, has_side_effects=True, vmem_limit_bytes=VMEM_BYTES
        ),
    )(grads, squares)


def weight_grad_kernel(left, right, out):
    out[0] = jnp.dot(left[...], right[...], preferred_element_type=jnp.float32)


def weight_grad_of(normed_t, grads):
    features, rows = normed_t.shape
    tile = grads.shape[1] // 3
    width = 256 if features % 256 == 0 else features
    return pl.pallas_call(
        weight_grad_kernel,
        grid=(3, features // width),
        out_shape=jax.ShapeDtypeStruct((3, features, tile), jnp.float32),
        in_specs=[
            pl.BlockSpec((width, rows), lambda s, f: (f, 0)),
            pl.BlockSpec((rows, tile), lambda s, f: (0, s)),
        ],
        out_specs=pl.BlockSpec((1, width, tile), lambda s, f: (s, f, 0)),
    )(normed_t, grads)


def layer_norm(values):
    center = values - jnp.mean(values, axis=-1, keepdims=True)
    spread = jnp.mean(center * center, axis=-1, keepdims=True)
    return center * lax.rsqrt(spread + 1e-06)


def norm_grad(values, cotangent):
    return jax.vjp(layer_norm, values)[1](cotangent)[0]


def attend_block(query_raw, key_raw, value_rows, segment, target):
    inverse_root = 1.0 / math.sqrt(HD)
    query_normed = layer_norm(query_raw).astype(jnp.bfloat16)
    key_normed = layer_norm(key_raw).astype(jnp.bfloat16)
    scores = (
        jnp.einsum("qhd,khd->hqk", query_normed, key_normed, preferred_element_type=jnp.float32)
        * inverse_root
    )
    valid = segment >= 0
    allowed = (segment[:, None] == segment[None, :]) & valid[:, None]
    exponent = jnp.where(allowed[None], jnp.exp(scores), 0.0)
    denominator = jnp.sum(exponent, axis=-1, keepdims=True)
    denominator = jnp.where(valid[None, :, None], denominator, 1.0)
    weights = (exponent / denominator).astype(jnp.bfloat16)
    attended = jnp.einsum("hqk,khd->qhd", weights, value_rows, preferred_element_type=jnp.float32)
    feature_count = attended.shape[1] * attended.shape[2]
    error_rows = jnp.where(
        valid[:, None], attended.reshape(-1, feature_count) - target.astype(jnp.float32), 0.0
    )
    squared_sum = jnp.sum(error_rows * error_rows)
    return (query_normed, key_normed, weights, error_rows, squared_sum)


def attend_back(
    query_raw, key_raw, query_normed, key_normed, value_rows, weights, error_rows, patch_total
):
    inverse_root = 1.0 / math.sqrt(HD)
    out_grad = (error_rows / patch_total).astype(jnp.bfloat16).reshape(query_normed.shape)
    prob_grad = jnp.einsum("qhd,khd->hqk", out_grad, value_rows, preferred_element_type=jnp.float32)
    value_grad = jnp.einsum(
        "hqk,qhd->khd", weights, out_grad, preferred_element_type=jnp.float32
    ).astype(jnp.bfloat16)
    weight_float = weights.astype(jnp.float32)
    score_grad = (
        weight_float
        * (prob_grad - jnp.sum(prob_grad * weight_float, axis=-1, keepdims=True))
        * inverse_root
    ).astype(jnp.bfloat16)
    normed_grad_q = jnp.einsum(
        "hqk,khd->qhd", score_grad, key_normed, preferred_element_type=jnp.float32
    )
    normed_grad_k = jnp.einsum(
        "hqk,qhd->khd", score_grad, query_normed, preferred_element_type=jnp.float32
    )
    query_grad = norm_grad(query_raw, normed_grad_q).astype(jnp.bfloat16)
    key_grad = norm_grad(key_raw, normed_grad_k).astype(jnp.bfloat16)
    return jnp.stack([query_grad, key_grad, value_grad], axis=1)


def local(n, n_mp, patches, embed_weight, project_weight, patch_counts, segment_ids, targets):
    counts = jnp.broadcast_to(jnp.sum(patch_counts).astype(jnp.float32), (8, 128))
    row_total = patches.shape[0]
    normed_t, projected, total = project(
        patches, embed_weight, jnp.transpose(project_weight, (1, 0, 2)), counts, n, n_mp
    )
    patch_total = total[0, 0]
    head_dev = project_weight.shape[2] // HD
    projected = projected.reshape(row_total, 3, head_dev, HD)
    query_raw = projected[:, 0]
    key_raw = projected[:, 1]
    value_rows = projected[:, 2].astype(jnp.bfloat16)
    query_normed, key_normed, weights, error_rows, squared_sum = attend_block(
        query_raw, key_raw, value_rows, segment_ids, targets
    )
    grad_rows = attend_back(
        query_raw, key_raw, query_normed, key_normed, value_rows, weights, error_rows, patch_total
    )
    gathered, squares = spread(
        grad_rows.reshape(row_total, -1), jnp.broadcast_to(squared_sum, (8, 128)), n, n_mp
    )
    loss_value = squares[0, 0] / (2.0 * patch_total)
    weight_grad = weight_grad_of(normed_t, gathered.reshape(-1, gathered.shape[2]))
    return (jnp.transpose(weight_grad, (1, 0, 2)), loss_value)


def solution(mesh):
    in_specs = (
        P("dp", None),
        P(("mp", "dp"), None),
        P("dp", None, "mp"),
        P("dp"),
        P("dp"),
        P("dp", "mp"),
    )
    out_specs = (P("dp", None, "mp"), P())
    return jax.shard_map(
        functools.partial(local, mesh.shape["dp"], mesh.shape["mp"]), mesh=mesh, in_specs=in_specs, out_specs=out_specs, check_vma=False)
```

```python
import functools
import math

import jax
import jax.numpy as jnp
from jax import lax
from jax.experimental import pallas as pl
from jax.experimental.pallas import tpu as pltpu
from jax.sharding import PartitionSpec as P

HD = 128
MESH = pl.DeviceIdType.MESH
VMEM_BYTES = 62 * 1024 * 1024


def remote(src, dst, send_sem, recv_sem, device_id):
    return pltpu.make_async_remote_copy(
        src_ref=src, dst_ref=dst, send_sem=send_sem, recv_sem=recv_sem,
        device_id=device_id, device_id_type=MESH,
    )


def greet(n, n_mp, d, m):
    barrier = pltpu.get_barrier_semaphore()
    for i in range(1, n):
        pl.semaphore_signal(barrier, inc=1, device_id={"dp": lax.rem(d + i, n)}, device_id_type=MESH)
    for i in range(1, n_mp):
        pl.semaphore_signal(barrier, inc=1, device_id={"mp": lax.rem(m + i, n_mp)}, device_id_type=MESH)
    pl.semaphore_wait(barrier, n - 1 + n_mp - 1)


def project_kernel(
    n, n_mp,
    patches, embed, weight_hbm, counts,
    normed_t, raw, total,
    normed, pall, zbuf, eblk, wbuf, stats, cbuf, pbuf, pin, sbuf, rbuf,
    w_sem, cs, cr, ps, pr, fs, fr, zs, zr, es, er, ss, sr, bs, br, qs, qr, loc_sem,
):
    d, m = lax.axis_index("dp"), lax.axis_index("mp")
    core, chip = lax.rem(d, 2), d // 2
    partner = d + 1 - 2 * core
    nc, per = n // 2, n // n_mp
    rows = patches.shape[0]
    tile = weight_hbm.shape[2]

    load = pltpu.make_async_copy(weight_hbm, wbuf, w_sem)
    load.start()
    greet(n, n_mp, d, m)

    def peer(i):
        return 2 * lax.rem(chip + i, nc) + core

    def source(i):
        return 2 * lax.rem(chip + nc - i, nc) + core

    def far(i):
        return lax.rem(d + i, n)

    def z_copy(i):
        return remote(embed, zbuf.at[i], zs.at[i], zr.at[i], {"mp": lax.rem(m + i, n_mp)})

    for i in range(1, n_mp):
        z_copy(i).start()

    def c_copy(i):
        return remote(counts, cbuf.at[i], cs.at[i], cr.at[i], {"dp": far(i)})

    def p_copy(i):
        return remote(patches, pall.at[d], ps.at[i], pr.at[i], {"dp": peer(i)})

    def p_own():
        return remote(patches, pall.at[d], ps.at[0], pr.at[0], {"dp": partner})

    def f_copy(i):
        return remote(pall.at[source(i)], pall.at[source(i)], fs.at[i], fr.at[i], {"dp": partner})

    def e_target(i):
        return lax.rem(m + n_mp - i, n_mp) * per + d // n_mp

    def e_copy(i, src):
        return remote(src, eblk.at[lax.rem(d, n_mp)], es.at[i], er.at[lax.rem(d, n_mp)], {"dp": e_target(i)})

    def e_local(i, src):
        return pltpu.make_async_copy(src, eblk.at[lax.rem(d, n_mp)], loc_sem)

    def e_start(i, src):
        @pl.when(e_target(i) != d)
        def _():
            e_copy(i, src).start()

        @pl.when(e_target(i) == d)
        def _():
            e_local(i, src).start()
            e_local(i, src).wait()

    p_own().start()
    for i in range(1, nc):
        p_copy(i).start()
    for i in range(1, n):
        c_copy(i).start()
    e_start(0, embed)
    pall[d] = patches[...]
    for i in range(1, nc):
        p_copy(i).wait_recv()
        f_copy(i).start()
    for i in range(1, n_mp):
        z_copy(i).wait_recv()
        e_start(i, zbuf.at[i])
    sum_counts = counts[...]
    for i in range(1, n):
        c_copy(i).wait_recv()
        sum_counts = sum_counts + cbuf[i]
    total[...] = sum_counts
    p_own().wait_recv()
    for i in range(1, nc):
        f_copy(i).wait_recv()
    for q in range(n_mp):
        origin = lax.rem(d, per) * n_mp + q

        @pl.when(origin != d)
        def _():
            remote(eblk.at[q], eblk.at[q], es.at[q], er.at[q], {"dp": partner}).wait_recv()

    width = eblk.shape[0] * eblk.shape[1]
    feature_total = width * n
    lane = lax.broadcasted_iota(jnp.int32, (rows, 128), 1)

    def embed_block(b, carry):
        block = pall[b]
        parts = jnp.concatenate(
            [eblk[q] for q in range(n_mp)], axis=0
        )
        value = lax.dot_general(
            block, parts, (((1,), (1,)), ((), ())), preferred_element_type=jnp.float32
        ).astype(jnp.bfloat16)
        normed[b] = value
        value = value.astype(jnp.float32)
        mean = jnp.sum(value, axis=-1, keepdims=True) * (1.0 / width)
        center = value - mean
        square = jnp.sum(center * center, axis=-1, keepdims=True)
        both = jnp.where(lane == 0, mean, jnp.where(lane == 1, square, 0.0))
        stats[0, b] = both.T[:8]
        return carry

    lax.fori_loop(0, n, embed_block, 0)

    def s_copy(i):
        return remote(stats.at[0], stats.at[i], ss.at[i], sr.at[i], {"dp": far(i)})

    for i in range(1, n):
        s_copy(i).start()
    for i in range(1, n):
        s_copy(i).wait_recv()

    load.wait()

    def norm_block(b, carry):
        mean = stats[0, b, 0:1, :]
        for i in range(1, n):
            mean = mean + stats[i, b, 0:1, :]
        mean = mean * (1.0 / n)
        square = jnp.zeros_like(mean)
        for i in range(n):
            gap = stats[i, b, 0:1, :] - mean
            square = square + stats[i, b, 1:2, :] + width * (gap * gap)
        scale = lax.rsqrt(square * (1.0 / feature_total) + 1e-06)
        row = lax.broadcasted_iota(jnp.int32, (128, rows), 0)
        both = jnp.where(row == 0, mean, jnp.where(row == 1, scale, 0.0)).T
        value = normed[b].astype(jnp.float32)
        normed[b] = ((value - both[:, 0:1]) * both[:, 1:2]).astype(jnp.bfloat16)
        return carry

    lax.fori_loop(0, n, norm_block, 0)

    def b_copy(i):
        return remote(pbuf.at[i], pin.at[i], bs.at[i], br.at[i], {"dp": partner})

    def q_copy(i):
        return remote(sbuf.at[i], rbuf.at[i], qs.at[i], qr.at[i], {"dp": peer(i)})

    def other_part(k, carry):
        i = lax.rem(k + 1, nc)
        block = normed[2 * lax.rem(chip + i, nc) + 1 - core]
        for s in range(3):
            pbuf[i, :, s * tile:(s + 1) * tile] = jnp.dot(
                block, wbuf[s], preferred_element_type=jnp.float32
            ).astype(jnp.bfloat16)
        b_copy(i).start()
        return carry

    lax.fori_loop(0, nc, other_part, 0)

    def own_part(i, carry):
        block = normed[peer(i)]
        b_copy(i).wait_recv()
        for s in range(3):
            cols = slice(s * tile, (s + 1) * tile)
            sbuf[i, :, cols] = (
                jnp.dot(block, wbuf[s], preferred_element_type=jnp.float32)
                + pin[i, :, cols].astype(jnp.float32)
            ).astype(jnp.bfloat16)
        q_copy(i).start()
        return carry

    lax.fori_loop(1, nc, own_part, 0)
    block = normed[d]
    b_copy(0).wait_recv()
    for s in range(3):
        cols = slice(s * tile, (s + 1) * tile)
        raw[:, cols] = jnp.dot(block, wbuf[s], preferred_element_type=jnp.float32) + pin[
            0, :, cols
        ].astype(jnp.float32)

    for b in range(n):
        normed_t[:, b * rows:(b + 1) * rows] = normed[b].T

    def take(i, carry):
        q_copy(i).wait_recv()
        raw[...] += rbuf[i].astype(jnp.float32)
        return carry

    lax.fori_loop(1, nc, take, 0)

    p_own().wait_send()
    for i in range(1, n_mp):
        z_copy(i).wait_send()
    for i in range(n_mp):
        @pl.when(e_target(i) != d)
        def _():
            e_copy(i, embed).wait_send()
    for i in range(1, nc):
        p_copy(i).wait_send()
        f_copy(i).wait_send()
        q_copy(i).wait_send()
    for i in range(nc):
        b_copy(i).wait_send()
    for i in range(1, n):
        c_copy(i).wait_send()
        s_copy(i).wait_send()


def project(patches, embed, weight, counts, n, n_mp):
    rows, width = patches.shape
    pieces = embed.shape[0]
    features, columns = weight.shape[1], 3 * weight.shape[2]
    nc = n // 2
    dma = lambda k: pltpu.SemaphoreType.DMA((k,))
    vmem = pl.BlockSpec(memory_space=pltpu.VMEM)
    bf16, f32 = jnp.bfloat16, jnp.float32
    return pl.pallas_call(
        functools.partial(project_kernel, n, n_mp),
        out_shape=(
            jax.ShapeDtypeStruct((features, n * rows), bf16),
            jax.ShapeDtypeStruct((rows, columns), f32),
            jax.ShapeDtypeStruct((8, 128), f32),
        ),
        in_specs=[vmem, vmem, pl.BlockSpec(memory_space=pl.ANY), vmem],
        out_specs=(vmem, vmem, vmem),
        scratch_shapes=[
            pltpu.VMEM((n, rows, features), bf16),
            pltpu.VMEM((n, rows, width), bf16),
            pltpu.VMEM((n_mp, pieces, width), bf16),
            pltpu.VMEM((n_mp, pieces, width), bf16),
            pltpu.VMEM(weight.shape, bf16),
            pltpu.VMEM((n, n, 8, rows), f32),
            pltpu.VMEM((n, 8, 128), f32),
            pltpu.VMEM((nc, rows, columns), bf16),
            pltpu.VMEM((nc, rows, columns), bf16),
            pltpu.VMEM((nc, rows, columns), bf16),
            pltpu.VMEM((nc, rows, columns), bf16),
            pltpu.SemaphoreType.DMA,
            dma(n), dma(n), dma(nc), dma(nc), dma(nc), dma(nc), dma(n_mp), dma(n_mp),
            dma(n_mp), dma(n_mp), dma(n), dma(n), dma(nc), dma(nc), dma(nc), dma(nc),
            pltpu.SemaphoreType.DMA,
        ],
        compiler_params=pltpu.CompilerParams(
            collective_id=0, has_side_effects=True, vmem_limit_bytes=VMEM_BYTES
        ),
    )(patches, embed, weight, counts)


def grid_side(nc):
    side = math.isqrt(nc)
    assert side * side == nc
    return side


def chip_at(chip, side, h, i, j):
    a, b = chip // side, lax.rem(chip, side)
    da, db = (j, i) if h == 0 else (i, j)
    return lax.rem(a + da + side, side) * side + lax.rem(b + db + side, side)


def spread_kernel(n, n_mp, chunks, grads, squares, gathered, loss, zsq, psq, mine, ps, pr, gs, gr, fs, fr, zs, zr, cs, cr, loc_sem):
    d, m = lax.axis_index("dp"), lax.axis_index("mp")
    core, chip = lax.rem(d, 2), d // 2
    partner = d + 1 - 2 * core
    nc = n // 2
    side = grid_side(nc)
    span = grads.shape[0] // chunks
    greet(n, n_mp, d, m)

    def part(k):
        return pl.ds(k * span, span)

    def block(k, i, j):
        if i == 0 and j == 0:
            return grads.at[part(k)]
        return gathered.at[2 * chip_at(chip, side, k % 2, -i, -j) + core, part(k)]

    def landing(k, i, j):
        return gathered.at[2 * chip_at(chip, side, k % 2, -i, -j) + core, part(k)]

    def first(k, i):
        to = 2 * chip_at(chip, side, k % 2, i, 0) + core
        return remote(block(k, 0, 0), landing(k, 0, 0), ps.at[k, i], pr.at[k, i], {"dp": to})

    def second(k, i, j):
        to = 2 * chip_at(chip, side, k % 2, 0, j) + core
        return remote(block(k, i, 0), landing(k, i, 0), gs.at[k, i, j], gr.at[k, i, j], {"dp": to})

    def across(k, i, j):
        return remote(block(k, i, j), landing(k, i, j), fs.at[k, i, j], fr.at[k, i, j], {"dp": partner})

    def z_copy(i):
        return remote(squares, zsq.at[i], zs.at[i], zr.at[i], {"mp": lax.rem(m + i, n_mp)})

    def c_copy(i):
        return remote(mine, psq.at[i], cs.at[i], cr.at[i], {"dp": lax.rem(d + i, n)})

    for i in range(1, n_mp):
        z_copy(i).start()
    for k in range(chunks):
        for i in range(1, side):
            first(k, i).start()
    for k in range(chunks):
        for j in range(1, side):
            second(k, 0, j).start()
        across(k, 0, 0).start()
    own = pltpu.make_async_copy(grads, gathered.at[d], loc_sem)
    own.start()
    value = squares[...]
    for i in range(1, n_mp):
        z_copy(i).wait_recv()
        value = value + zsq[i]
    mine[...] = value
    for i in range(1, n):
        c_copy(i).start()
    for k in range(chunks):
        for i in range(1, side):
            first(k, i).wait_recv()
            for j in range(1, side):
                second(k, i, j).start()
            across(k, i, 0).start()
    for i in range(1, n):
        c_copy(i).wait_recv()
        value = value + psq[i]
    loss[...] = value
    for i in range(side):
        for k in range(chunks):
            for j in range(1, side):
                second(k, i, j).wait_recv()
                across(k, i, j).start()
    own.wait()
    for k in range(chunks):
        for i in range(side):
            if i:
                first(k, i).wait_send()
            for j in range(side):
                if j:
                    second(k, i, j).wait_send()
                across(k, i, j).wait()
    for i in range(1, n_mp):
        z_copy(i).wait_send()
    for i in range(1, n):
        c_copy(i).wait_send()


def spread(grads, squares, n, n_mp):
    chunks = 4
    side = grid_side(n // 2)
    dma = lambda *k: pltpu.SemaphoreType.DMA(k)
    vmem = pl.BlockSpec(memory_space=pltpu.VMEM)
    return pl.pallas_call(
        functools.partial(spread_kernel, n, n_mp, chunks),
        out_shape=(
            jax.ShapeDtypeStruct((n,) + grads.shape, grads.dtype),
            jax.ShapeDtypeStruct((8, 128), jnp.float32),
        ),
        in_specs=[vmem, vmem],
        out_specs=(vmem, vmem),
        scratch_shapes=[
            pltpu.VMEM((n_mp, 8, 128), jnp.float32),
            pltpu.VMEM((n, 8, 128), jnp.float32),
            pltpu.VMEM((8, 128), jnp.float32),
            dma(chunks, side), dma(chunks, side),
            dma(chunks, side, side), dma(chunks, side, side),
            dma(chunks, side, side), dma(chunks, side, side),
            dma(n_mp), dma(n_mp), dma(n), dma(n),
            pltpu.SemaphoreType.DMA,
        ],
        compiler_params=pltpu.CompilerParams(
            collective_id=1, has_side_effects=True, vmem_limit_bytes=VMEM_BYTES
        ),
    )(grads, squares)


def weight_grad_kernel(left, right, out):
    out[0] = jnp.dot(left[...], right[...], preferred_element_type=jnp.float32)


def weight_grad_of(normed_t, grads):
    features, rows = normed_t.shape
    tile = grads.shape[1] // 3
    half = tile // 2 if tile % 256 == 0 else tile
    return pl.pallas_call(
        weight_grad_kernel,
        grid=(3, tile // half),
        out_shape=jax.ShapeDtypeStruct((3, features, tile), jnp.float32),
        in_specs=[
            pl.BlockSpec((features, rows), lambda s, f: (0, 0)),
            pl.BlockSpec((rows, half), lambda s, f: (0, s * (tile // half) + f)),
        ],
        out_specs=pl.BlockSpec((1, features, half), lambda s, f: (s, 0, f)),
    )(normed_t, grads)


def layer_norm(values):
    center = values - jnp.mean(values, axis=-1, keepdims=True)
    spread = jnp.mean(center * center, axis=-1, keepdims=True)
    return center * lax.rsqrt(spread + 1e-06)


def norm_grad(values, cotangent):
    return jax.vjp(layer_norm, values)[1](cotangent)[0]


def attend_block(query_raw, key_raw, value_rows, segment, target):
    inverse_root = 1.0 / math.sqrt(HD)
    query_normed = layer_norm(query_raw).astype(jnp.bfloat16)
    key_normed = layer_norm(key_raw).astype(jnp.bfloat16)
    scores = (
        jnp.einsum("qhd,khd->hqk", query_normed, key_normed, preferred_element_type=jnp.float32)
        * inverse_root
    )
    valid = segment >= 0
    allowed = (segment[:, None] == segment[None, :]) & valid[:, None]
    exponent = jnp.where(allowed[None], jnp.exp(scores), 0.0)
    denominator = jnp.sum(exponent, axis=-1, keepdims=True)
    denominator = jnp.where(valid[None, :, None], denominator, 1.0)
    weights = (exponent / denominator).astype(jnp.bfloat16)
    attended = jnp.einsum("hqk,khd->qhd", weights, value_rows, preferred_element_type=jnp.float32)
    feature_count = attended.shape[1] * attended.shape[2]
    error_rows = jnp.where(
        valid[:, None], attended.reshape(-1, feature_count) - target.astype(jnp.float32), 0.0
    )
    squared_sum = jnp.sum(error_rows * error_rows)
    return (query_normed, key_normed, weights, error_rows, squared_sum)


def attend_back(
    query_raw, key_raw, query_normed, key_normed, value_rows, weights, error_rows, patch_total
):
    inverse_root = 1.0 / math.sqrt(HD)
    out_grad = (error_rows / patch_total).astype(jnp.bfloat16).reshape(query_normed.shape)
    prob_grad = jnp.einsum("qhd,khd->hqk", out_grad, value_rows, preferred_element_type=jnp.float32)
    value_grad = jnp.einsum(
        "hqk,qhd->khd", weights, out_grad, preferred_element_type=jnp.float32
    ).astype(jnp.bfloat16)
    weight_float = weights.astype(jnp.float32)
    score_grad = (
        weight_float
        * (prob_grad - jnp.sum(prob_grad * weight_float, axis=-1, keepdims=True))
        * inverse_root
    ).astype(jnp.bfloat16)
    normed_grad_q = jnp.einsum(
        "hqk,khd->qhd", score_grad, key_normed, preferred_element_type=jnp.float32
    )
    normed_grad_k = jnp.einsum(
        "hqk,qhd->khd", score_grad, query_normed, preferred_element_type=jnp.float32
    )
    query_grad = norm_grad(query_raw, normed_grad_q).astype(jnp.bfloat16)
    key_grad = norm_grad(key_raw, normed_grad_k).astype(jnp.bfloat16)
    return jnp.stack([query_grad, key_grad, value_grad], axis=1)


def local(n, n_mp, patches, embed_weight, project_weight, patch_counts, segment_ids, targets):
    counts = jnp.broadcast_to(jnp.sum(patch_counts).astype(jnp.float32), (8, 128))
    row_total = patches.shape[0]
    normed_t, projected, total = project(
        patches, embed_weight, jnp.transpose(project_weight, (1, 0, 2)), counts, n, n_mp
    )
    patch_total = total[0, 0]
    head_dev = project_weight.shape[2] // HD
    projected = projected.reshape(row_total, 3, head_dev, HD)
    query_raw = projected[:, 0]
    key_raw = projected[:, 1]
    value_rows = projected[:, 2].astype(jnp.bfloat16)
    query_normed, key_normed, weights, error_rows, squared_sum = attend_block(
        query_raw, key_raw, value_rows, segment_ids, targets
    )
    grad_rows = attend_back(
        query_raw, key_raw, query_normed, key_normed, value_rows, weights, error_rows, patch_total
    )
    gathered, squares = spread(
        grad_rows.reshape(row_total, -1), jnp.broadcast_to(squared_sum, (8, 128)), n, n_mp
    )
    loss_value = squares[0, 0] / (2.0 * patch_total)
    weight_grad = weight_grad_of(normed_t, gathered.reshape(-1, gathered.shape[2]))
    return (jnp.transpose(weight_grad, (1, 0, 2)), loss_value)


def solution(mesh):
    in_specs = (
        P("dp", None),
        P(("mp", "dp"), None),
        P("dp", None, "mp"),
        P("dp"),
        P("dp"),
        P("dp", "mp"),
    )
    out_specs = (P("dp", None, "mp"), P())
    return jax.shard_map(
        functools.partial(local, mesh.shape["dp"], mesh.shape["mp"]), mesh=mesh, in_specs=in_specs, out_specs=out_specs, check_vma=False)
```
